32 devices in a mesh: groups: 2 (over y), seq: 4 (over z), mp: 2 (over x), rep: 2 (over core).
Axes of the slice: x: 2, y: 2, z: 4, core: 2. Of those that a mesh axis runs over, the one named last changes fastest.
Arguments:
- encoder_rows: bfloat16 [8, 512, 4096], P('groups', ('seq', 'rep'), 'mp'), parts along dimension 0
- norm_gain: bfloat16 [4096], replicated, may hold values from 0.099609375 to 1.8984375
- key_weight: bfloat16 [4096, 2048], P(None, 'mp'), may hold values from -0.09375 to 0.09375
- value_weight: bfloat16 [4096, 2048], P(None, 'mp'), may hold values from -0.09375 to 0.09375
- queries: bfloat16 [64, 512, 2048], P(('groups', 'seq', 'rep'), None, 'mp'), parts along dimension 0
- wild_lengths: int32 [8], P('groups'), parts along dimension 0, may hold values from 128 to 512, as said below
- variant_counts: int32 [8], P('groups'), parts along dimension 0, may hold values from 4 to 12, as said below
Outputs:
- context: bfloat16 [64, 512, 2048], P(('groups', 'seq', 'rep'), None, 'mp'), parts along dimension 0
The draws below stay inside these ranges and needn't reach their ends.
There are 2 independent parts, one for each index of `groups`. The reference program is written for one: setup_inputs(seed, part) draws one part's arguments, and reference() takes and returns one part's arrays. A program takes and returns all parts, laid end to end along the dimension named above; an argument that names none is the same for every part. Nothing has to cross between parts.
Inputs may be any that keep to these rules, and one draw needn't show every extreme that they name: `variant_counts`: the counts sum to 32; every wild type has at least 4 and at most 12 variants, and both ends are reached. Variants fill the slots in order of wild type, 4 slots to a device in the order of seq+rep, so one device's slots name at most two wild types; when 4 > 1 some device's slots name two. `wild_lengths`: some wild type has length 512.
All inputs are finite; a program needn't handle non-finite values.
Results may differ from the reference program's by a relative error of at most 0.0018.
The reference program's roundings to bfloat16 on the way count: a program that leaves them out, or rounds other values in their place, can miss the bound.
Values may be sent and summed in bfloat16 or wider, within the bound.
A program may use at most 128 MiB of HBM per device.

```python
import math
import jax
import jax.numpy as jnp
from jax import lax

D = 4096
HEADS = 32
HD = 64
LEN = 512
VARIANT_SLOTS = 4
WILD = 4
VARS = 32
INNER = 2048


def draw_encoder_rows(key, part):
    noise_key, scale_key = jax.random.split(jax.random.fold_in(key, 7))
    ramp = jnp.sqrt(1.0 + 2.0 * jnp.arange(D, dtype=jnp.float32) / (D - 1))
    row_scale = jnp.exp(jax.random.uniform(scale_key, (WILD, LEN, 1), minval=0.0, maxval=math.log(10.0)))
    base = jax.random.normal(noise_key, (WILD, LEN, D))
    return (base * ramp[None, None, :] * row_scale).astype(jnp.bfloat16)


def draw_queries(key, part):
    noise_key = jax.random.fold_in(jax.random.fold_in(key, 5), 0)
    return (0.3 * jax.random.normal(noise_key, (VARS, LEN, INNER))).astype(jnp.bfloat16)


def draw_wild_lengths(key, part):
    length_key, place_key = jax.random.split(jax.random.fold_in(key, 9))
    drawn = jax.random.randint(length_key, (WILD,), LEN // 4, LEN + 1)
    longest = jax.random.randint(place_key, (), 0, WILD)
    return jnp.where(jnp.arange(WILD) == longest, LEN, drawn).astype(jnp.int32)


def draw_variant_counts(key, part):
    sorting_key, reward_key = jax.random.split(jax.random.fold_in(key, 3))
    couple_count = WILD // 2
    ranking = jax.random.permutation(sorting_key, WILD).astype(jnp.int32)
    number = jnp.arange(WILD, dtype=jnp.int32)
    place = jnp.sum(jnp.where(ranking[None, :] == number[:, None], number[None, :], 0), axis=1).astype(jnp.int32)
    couple_lookup = place // 2
    half_lookup = place % 2
    extra_reward = jax.random.randint(reward_key, (couple_count,), 0, 2 * VARIANT_SLOTS + 1).astype(jnp.int32)
    couple_number = jnp.arange(couple_count, dtype=jnp.int32)
    leading_couple = couple_lookup[0]
    leading_half = half_lookup[0]
    broadest_couple = (leading_couple + 1) % couple_count
    leading_reward = jnp.where(leading_half == 0, 1, 2 * VARIANT_SLOTS - 1).astype(jnp.int32)
    extra_reward = jnp.where(couple_number == broadest_couple, 2 * VARIANT_SLOTS, extra_reward)
    extra_reward = jnp.where(couple_number == leading_couple, leading_reward, extra_reward)
    self_reward = extra_reward[couple_lookup]
    portion_amount = jnp.where(half_lookup == 0, self_reward, 2 * VARIANT_SLOTS - self_reward)
    return (VARIANT_SLOTS + portion_amount).astype(jnp.int32)


def level_of(own_key, shape, cuts, least, largest):
    gain, own = 1.0, jax.random.fold_in(own_key, 6)
    for axis_at, parts in cuts:
        steps = jnp.exp(jax.random.uniform(jax.random.fold_in(own, axis_at), (parts,), jnp.float32, least / len(cuts), largest / len(cuts)))
        gain = gain * jnp.repeat(steps, shape[axis_at] // parts).reshape([-1 if axis == axis_at else 1 for axis in range(len(shape))])
    return gain


def normal_values(stream_key, extent, width, bound, cuts=(), kind=jnp.bfloat16):
    result = jax.random.normal(stream_key, extent, jnp.float32) * width
    if len(cuts) > 0:
        result = level_of(stream_key, extent, cuts, -0.22, 0.18) * result
    return jnp.clip(result, min=-bound, max=bound).astype(kind)


def setup_inputs(seed: int = 0, part: int = 0) -> dict:
    seeds = jax.random.split(jax.random.key(seed), 8)
    part_splits = jax.random.split(jax.random.fold_in(seeds[7], part), 8)
    return {
        "encoder_rows": draw_encoder_rows(jax.random.fold_in(jax.random.fold_in(seeds[7], part), 71), part),
        "norm_gain": jnp.clip(1.0 + 0.18 * jax.random.normal(seeds[1], (D,), jnp.float32), 0.099609375, 1.8984375).astype(jnp.bfloat16),
        "key_weight": normal_values(seeds[2], (D, INNER), D ** -0.5, 0.09375, ((1, 2),)),
        "value_weight": normal_values(seeds[3], (D, INNER), D ** -0.5, 0.09375, ((1, 2),)),
        "queries": draw_queries(jax.random.fold_in(jax.random.fold_in(seeds[7], part), 71), part),
        "wild_lengths": draw_wild_lengths(jax.random.fold_in(jax.random.fold_in(seeds[7], part), 71), part),
        "variant_counts": draw_variant_counts(jax.random.fold_in(jax.random.fold_in(seeds[7], part), 71), part),
    }


def wild_of_slots(variant_counts, slot_total):
    running_end = jnp.cumsum(variant_counts).astype(jnp.int32)
    slot_number = jnp.arange(slot_total, dtype=jnp.int32)
    return lax.optimization_barrier(jnp.sum((running_end[None, :] <= slot_number[:, None]).astype(jnp.int32), axis=1)).astype(jnp.int32)

def reference(encoder_rows, norm_gain, key_weight, value_weight, queries, wild_lengths, variant_counts):
    slot_wild = wild_of_slots(variant_counts, VARS)
    flat_rows = encoder_rows.reshape(WILD * LEN, D).astype(jnp.float32)
    mean_square = lax.optimization_barrier(jnp.mean(flat_rows * flat_rows, axis=1))
    gained = (flat_rows * norm_gain.astype(jnp.float32)[None, :]).astype(jnp.bfloat16)
    inverse_rms = lax.rsqrt(mean_square + 1e-06)[:, None]
    key_rows = (inverse_rms * jnp.dot(gained, key_weight, preferred_element_type=jnp.float32)).astype(jnp.bfloat16)
    value_rows = (inverse_rms * jnp.dot(gained, value_weight, preferred_element_type=jnp.float32)).astype(jnp.bfloat16)
    key_heads = key_rows.reshape(WILD, LEN, HEADS, HD)
    value_heads = value_rows.reshape(WILD, LEN, HEADS, HD)
    positions = jnp.arange(LEN, dtype=jnp.int32)

    def attend_slot(packed):
        query_rows, wild_index = packed
        seq_length = wild_lengths[wild_index]
        query_heads = query_rows.reshape(LEN, HEADS, HD).astype(jnp.float32)
        scores = jnp.einsum('qhd,khd->hqk', query_heads, key_heads[wild_index].astype(jnp.float32))
        validity = positions < seq_length
        scores = jnp.where(validity[None, None, :], scores, jnp.float32(-1e+30))
        maximum = lax.optimization_barrier(jnp.max(scores, axis=2, keepdims=True))
        weights = jnp.exp(scores - maximum)
        softmax_weights = (weights / lax.optimization_barrier(jnp.sum(weights, axis=2, keepdims=True))).astype(jnp.bfloat16)
        outcome = jnp.einsum('hqk,khd->qhd', softmax_weights.astype(jnp.float32), value_heads[wild_index].astype(jnp.float32))
        outcome = jnp.where(validity[:, None, None], outcome, jnp.float32(0.0))
        return outcome.reshape(LEN, INNER).astype(jnp.bfloat16)
    return lax.map(attend_slot, (queries, slot_wild))
```

```python
import functools

import jax
import jax.numpy as jnp
from jax import lax
from jax.experimental import pallas as pl
from jax.experimental.pallas import tpu as pltpu
from jax.sharding import PartitionSpec as P

D = 4096
HD = 64
LEN = 512
PAIR = 2 * HD
Q_CHUNK = 256
HEAD_CHUNKS = 2


def wild_of_slots(variant_counts, slot_total):
    running_end = jnp.cumsum(variant_counts)
    slot_number = jnp.arange(slot_total, dtype=jnp.int32)
    return jnp.sum((running_end[None, :] <= slot_number[:, None]).astype(jnp.int32), axis=1)


def attend_kernel(wild_ref, length_ref, q_ref, k_ref, v_ref, *rest):
    o_ref = rest[-1]
    length = length_ref[pl.program_id(1)]
    keys = k_ref[...].reshape(LEN, PAIR)
    values = v_ref[...].reshape(LEN, PAIR)
    lane = lax.broadcasted_iota(jnp.int32, (Q_CHUNK, PAIR), 1)
    valid = lax.broadcasted_iota(jnp.int32, (Q_CHUNK, LEN), 1) < length
    for start in range(0, LEN, Q_CHUNK):
        query = q_ref[0, pl.ds(start, Q_CHUNK), :]
        outs = []
        for head in range(2):
            own_lanes = lane < HD if head == 0 else lane >= HD
            masked_query = jnp.where(own_lanes, query, jnp.zeros_like(query))
            scores = lax.dot_general(
                masked_query, keys, (((1,), (1,)), ((), ())), preferred_element_type=jnp.float32
            )
            scores = jnp.where(valid, scores, jnp.float32(-1e30))
            maximum = jnp.max(scores, axis=1, keepdims=True)
            weights = jnp.exp(scores - maximum)
            inverse = 1.0 / jnp.sum(weights, axis=1, keepdims=True)
            probs = (weights * inverse).astype(jnp.bfloat16)
            outs.append(jnp.dot(probs, values, preferred_element_type=jnp.float32))
        out = jnp.where(lane < HD, outs[0], outs[1])
        row = start + lax.broadcasted_iota(jnp.int32, (Q_CHUNK, PAIR), 0)
        o_ref[0, pl.ds(start, Q_CHUNK), :] = jnp.where(row < length, out, 0.0).astype(o_ref.dtype)


def attend(own_wild, own_lengths, queries, gathered, previous, chunk):
    slots, _, inner = queries.shape
    peers, _, part, double = gathered.shape
    pairs = double // 2 // PAIR
    base = chunk * pairs
    kv_block = (peers, 1, part, PAIR)
    in_specs = [
        pl.BlockSpec((1, LEN, PAIR), lambda h, s, w, n: (s, 0, base + h)),
        pl.BlockSpec(kv_block, lambda h, s, w, n: (0, w[s], 0, h)),
        pl.BlockSpec(kv_block, lambda h, s, w, n: (0, w[s], 0, pairs + h)),
    ]
    operands = [own_wild, own_lengths, queries, gathered, gathered]
    aliases = {}
    if previous is not None:
        in_specs.append(pl.BlockSpec(memory_space=pl.ANY))
        operands.append(previous)
        aliases = {5: 0}
    elements = slots * pairs * 2 * LEN * LEN
    return pl.pallas_call(
        attend_kernel,
        out_shape=jax.ShapeDtypeStruct(queries.shape, jnp.bfloat16),
        grid_spec=pltpu.PrefetchScalarGridSpec(
            num_scalar_prefetch=2,
            grid=(pairs, slots),
            in_specs=in_specs,
            out_specs=pl.BlockSpec((1, LEN, PAIR), lambda h, s, w, n: (s, 0, base + h)),
        ),
        input_output_aliases=aliases,
        compiler_params=pltpu.CompilerParams(vmem_limit_bytes=32 << 20),
        cost_estimate=pl.CostEstimate(
            flops=elements * 2 * PAIR * 2, transcendentals=elements, bytes_accessed=slots * pairs * LEN * PAIR * 8
        ),
    )(*operands)


def local(encoder_rows, norm_gain, key_weight, value_weight, queries, wild_lengths, variant_counts):
    wild_total, part_length, part_width = encoder_rows.shape
    row_total = wild_total * part_length
    inner_local = key_weight.shape[1]
    seq_size = lax.axis_size("seq")
    rep_size = lax.axis_size("rep")
    peer_total = seq_size * rep_size
    slot_local = queries.shape[0]
    slot_wild = wild_of_slots(variant_counts, peer_total * slot_local)
    own_index = lax.axis_index("seq") * rep_size + lax.axis_index("rep")
    own_wild = lax.dynamic_slice_in_dim(slot_wild, own_index * slot_local, slot_local, 0)
    wild_number = jnp.arange(wild_total, dtype=jnp.int32)
    own_lengths = jnp.sum(
        jnp.where(own_wild[:, None] == wild_number[None, :], wild_lengths[None, :], 0), axis=1
    )
    own_wild = jnp.minimum(own_wild, wild_total - 1)
    rows = lax.all_gather(encoder_rows, "mp", axis=2, tiled=True).reshape(row_total, -1).astype(jnp.float32)
    gained = (rows * norm_gain.astype(jnp.float32)[None, :]).astype(jnp.bfloat16)
    inverse_rms = lax.rsqrt(jnp.sum(rows * rows, axis=1) / D + 1e-06)[:, None]
    width = inner_local // HEAD_CHUNKS
    shared = []
    for chunk in range(HEAD_CHUNKS):
        columns = slice(chunk * width, (chunk + 1) * width)
        parts = []
        for weight in (key_weight, value_weight):
            total = jnp.dot(gained, weight[:, columns], preferred_element_type=jnp.float32)
            parts.append((inverse_rms * total).astype(jnp.bfloat16))
        paired = jnp.concatenate(parts, axis=1).reshape(wild_total, part_length, 2 * width)
        shared.append(lax.all_gather(paired, ("seq", "rep"), axis=0))
    context = None
    for chunk in range(HEAD_CHUNKS):
        context = attend(own_wild, own_lengths, queries, shared[chunk], context, chunk)
    return context


def solution(mesh):
    placed = (
        P("groups", ("seq", "rep"), "mp"),
        P(),
        P(None, "mp"),
        P(None, "mp"),
        P(("groups", "seq", "rep"), None, "mp"),
        P("groups"),
        P("groups"),
    )
    return jax.shard_map(
        local,
        mesh=mesh,
        in_specs=placed,
        out_specs=P(("groups", "seq", "rep"), None, "mp"),
        check_vma=False,
    )
```

```python
import functools

import jax
import jax.numpy as jnp
from jax import lax
from jax.experimental import pallas as pl
from jax.experimental.pallas import tpu as pltpu
from jax.sharding import PartitionSpec as P

D = 4096
HD = 64
LEN = 512
PAIR = 2 * HD
Q_CHUNK = 256
HEAD_CHUNKS = 2
ROW_GROUPS = 2
PIECES = 4
COUNT_MIN = 4
COUNT_MAX = 12
MESH = pl.DeviceIdType.MESH


def wild_of_slots(variant_counts, slot_total):
    running_end = jnp.cumsum(variant_counts)
    slot_number = jnp.arange(slot_total, dtype=jnp.int32)
    return jnp.sum((running_end[None, :] <= slot_number[:, None]).astype(jnp.int32), axis=1)


def attend_kernel(wild_ref, length_ref, q_ref, k_ref, v_ref, *rest):
    o_ref = rest[-1]
    length = length_ref[pl.program_id(1)]
    keys = k_ref[...].reshape(LEN, PAIR)
    values = v_ref[...].reshape(LEN, PAIR)
    lane = lax.broadcasted_iota(jnp.int32, (Q_CHUNK, PAIR), 1)
    valid = lax.broadcasted_iota(jnp.int32, (Q_CHUNK, LEN), 1) < length
    for start in range(0, LEN, Q_CHUNK):
        query = q_ref[0, pl.ds(start, Q_CHUNK), :]
        outs = []
        for head in range(2):
            own_lanes = lane < HD if head == 0 else lane >= HD
            masked_query = jnp.where(own_lanes, query, jnp.zeros_like(query))
            scores = lax.dot_general(
                masked_query, keys, (((1,), (1,)), ((), ())), preferred_element_type=jnp.float32
            )
            scores = jnp.where(valid, scores, jnp.float32(-1e30))
            maximum = jnp.max(scores, axis=1, keepdims=True)
            weights = jnp.exp(scores - maximum)
            inverse = 1.0 / jnp.sum(weights, axis=1, keepdims=True)
            probs = (weights * inverse).astype(jnp.bfloat16)
            outs.append(jnp.dot(probs, values, preferred_element_type=jnp.float32))
        out = jnp.where(lane < HD, outs[0], outs[1])
        row = start + lax.broadcasted_iota(jnp.int32, (Q_CHUNK, PAIR), 0)
        o_ref[0, pl.ds(start, Q_CHUNK), :] = jnp.where(row < length, out, 0.0).astype(o_ref.dtype)


def attend(own_wild, own_lengths, queries, gathered):
    slots, _, inner = queries.shape
    chunks, peers, _, part, double = gathered.shape
    per_chunk = double // 2 // PAIR
    pairs = chunks * per_chunk
    kv_block = (1, peers, 1, part, PAIR)
    elements = slots * pairs * 2 * LEN * LEN
    return pl.pallas_call(
        attend_kernel,
        out_shape=jax.ShapeDtypeStruct(queries.shape, jnp.bfloat16),
        grid_spec=pltpu.PrefetchScalarGridSpec(
            num_scalar_prefetch=2,
            grid=(pairs, slots),
            in_specs=[
                pl.BlockSpec((1, LEN, PAIR), lambda h, s, w, n: (s, 0, h)),
                pl.BlockSpec(kv_block, lambda h, s, w, n: (h // per_chunk, 0, w[s], 0, h % per_chunk)),
                pl.BlockSpec(kv_block, lambda h, s, w, n: (h // per_chunk, 0, w[s], 0, per_chunk + h % per_chunk)),
            ],
            out_specs=pl.BlockSpec((1, LEN, PAIR), lambda h, s, w, n: (s, 0, h)),
        ),
        compiler_params=pltpu.CompilerParams(vmem_limit_bytes=32 << 20),
        cost_estimate=pl.CostEstimate(
            flops=elements * 2 * PAIR * 2, transcendentals=elements, bytes_accessed=slots * pairs * LEN * PAIR * 8
        ),
    )(own_wild, own_lengths, queries, gathered, gathered)


def exchange_kernel(
    sizes, x_ref, gain_ref, kw_ref, vw_ref, out_ref, x_full, weights, gained, scale, own,
    x_sems, w_sems, x_send, x_recv, z_send, z_recv, r_send, r_recv, o_sems,
):
    seq_size, mp_size, rep_size, slot_local, wild_total, part = sizes
    z, m, r = lax.axis_index("seq"), lax.axis_index("mp"), lax.axis_index("rep")
    row_total, part_width = x_ref.shape
    width = kw_ref.shape[1] // HEAD_CHUNKS
    group_rows = row_total // ROW_GROUPS
    piece_wilds = wild_total // PIECES
    group_pieces = PIECES // ROW_GROUPS
    group_wilds = wild_total // ROW_GROUPS
    chip_slots = slot_local * rep_size
    total_slots = chip_slots * seq_size

    barrier = pltpu.get_barrier_semaphore()
    for off in range(1, mp_size):
        pl.semaphore_signal(barrier, 1, device_id={"mp": lax.rem(m + off, mp_size)}, device_id_type=MESH)
    for off in range(1, rep_size):
        pl.semaphore_signal(barrier, 1, device_id={"rep": lax.rem(r + off, rep_size)}, device_id_type=MESH)

    @pl.when(z < seq_size - 1)
    def _():
        pl.semaphore_signal(barrier, 1, device_id={"seq": z + 1}, device_id_type=MESH)

    @pl.when(z > 0)
    def _():
        pl.semaphore_signal(barrier, 1, device_id={"seq": z - 1}, device_id_type=MESH)

    def rows_of(group):
        return pl.ds(group * group_rows, group_rows)

    def own_copy(group):
        return pltpu.make_async_copy(
            x_ref.at[rows_of(group)], x_full.at[m, rows_of(group)], x_sems.at[group]
        )

    def weight_copy(chunk, which):
        ref = (kw_ref, vw_ref)[which]
        return pltpu.make_async_copy(
            ref.at[:, pl.ds(chunk * width, width)], weights.at[chunk, which], w_sems.at[chunk, which]
        )

    def feature_copy(group, off, sender):
        return pltpu.make_async_remote_copy(
            src_ref=x_ref.at[rows_of(group)],
            dst_ref=x_full.at[sender, rows_of(group)],
            send_sem=x_send.at[group, off - 1],
            recv_sem=x_recv.at[group, off - 1],
            device_id={"mp": lax.rem(m + off, mp_size)},
            device_id_type=MESH,
        )

    for group in range(ROW_GROUPS):
        own_copy(group).start()
    for chunk in range(HEAD_CHUNKS):
        for which in range(2):
            weight_copy(chunk, which).start()
    neighbours = (mp_size - 1) + (rep_size - 1) + jnp.where(z > 0, 1, 0) + jnp.where(z < seq_size - 1, 1, 0)
    pl.semaphore_wait(barrier, neighbours)
    for group in range(ROW_GROUPS):
        for off in range(1, mp_size):
            feature_copy(group, off, m).start()

    def lowest(piece):
        wild = piece * piece_wilds
        return max(COUNT_MIN * wild, total_slots - COUNT_MAX * (wild_total - wild))

    def highest(piece):
        wild = (piece + 1) * piece_wilds
        return min(COUNT_MAX * wild, total_slots - COUNT_MIN * (wild_total - wild))

    def wanted_right(chip, piece):
        return highest(piece) > chip * chip_slots

    def wanted_left(chip, piece):
        return lowest(piece) < (chip + 1) * chip_slots

    def slab(chunk, origin, core, piece):
        return out_ref.at[chunk, origin, core, pl.ds(piece * piece_wilds, piece_wilds)]

    def own_slab(chunk, piece):
        return own.at[chunk, pl.ds(piece * piece_wilds, piece_wilds)]

    def hop(way, step, chunk, piece, origin, from_own):
        ahead = z + 1 if way == 0 else z - 1
        return pltpu.make_async_remote_copy(
            src_ref=own_slab(chunk, piece) if from_own else slab(chunk, origin, r, piece),
            dst_ref=slab(chunk, origin, r, piece),
            send_sem=z_send.at[way, step, chunk, piece],
            recv_sem=z_recv.at[way, step, chunk, piece],
            device_id={"seq": ahead},
            device_id_type=MESH,
        )

    def twin(off, way, step, chunk, piece, origin, core, from_own):
        return pltpu.make_async_remote_copy(
            src_ref=own_slab(chunk, piece) if from_own else slab(chunk, origin, core, piece),
            dst_ref=slab(chunk, origin, core, piece),
            send_sem=r_send.at[off - 1, way, step, chunk, piece],
            recv_sem=r_recv.at[off - 1, way, step, chunk, piece],
            device_id={"rep": lax.rem(r + off, rep_size)},
            device_id_type=MESH,
        )

    def origin_of(way, step):
        return z - step if way == 0 else z + step

    def sends(way, step, piece):
        if way == 0:
            return (z - step >= 0) & (z < seq_size - 1) & wanted_right(z + 1, piece)
        return (z + step < seq_size) & (z > 0) & wanted_left(z - 1, piece)

    def arrives(way, step, piece):
        if way == 0:
            return (z - step >= 0) & wanted_right(z, piece)
        return (z + step < seq_size) & wanted_left(z, piece)

    def twin_moves(way, step, piece):
        near = wanted_right(z, piece) & wanted_left(z, piece)
        return near if step == 0 else near & arrives(way, step, piece)

    def first_sends(group, chunk):
        for piece in range(group * group_pieces, (group + 1) * group_pieces):
            for way in range(2):
                pl.when(sends(way, 0, piece))(hop(way, 0, chunk, piece, z, True).start)
            for off in range(1, rep_size):
                pl.when(twin_moves(0, 0, piece))(twin(off, 0, 0, chunk, piece, z, r, True).start)
            pltpu.make_async_copy(
                own_slab(chunk, piece), slab(chunk, z, r, piece), o_sems.at[chunk, piece]
            ).start()

    def forward(group, chunk, step):
        for piece in range(group * group_pieces, (group + 1) * group_pieces):
            for way in range(2):
                origin = origin_of(way, step)

                @pl.when(arrives(way, step, piece))
                def _():
                    hop(way, step - 1, chunk, piece, origin, False).wait_recv()

                if step < seq_size - 1:
                    pl.when(sends(way, step, piece))(hop(way, step, chunk, piece, origin, False).start)
                for off in range(1, rep_size):
                    pl.when(twin_moves(way, step, piece))(
                        twin(off, way, step, chunk, piece, origin, r, False).start
                    )

    def project(group, chunk):
        rows = rows_of(group)
        if chunk == 0:
            own_copy(group).wait()
            for off in range(1, mp_size):
                feature_copy(group, off, lax.rem(m - off + mp_size, mp_size)).wait_recv()
            squares = jnp.zeros((group_rows, 1), jnp.float32)
            for block in range(mp_size):
                columns = pl.ds(block * part_width, part_width)
                wide = x_full[block, rows, :].astype(jnp.float32)
                squares = squares + jnp.sum(wide * wide, axis=1, keepdims=True)
                gained[:, columns] = (wide * gain_ref[:, columns]).astype(jnp.bfloat16)
            scale[...] = lax.rsqrt(squares / D + 1e-06)
        for which in range(2):
            if group == 0:
                weight_copy(chunk, which).wait()
            total = jnp.dot(gained[...], weights[chunk, which], preferred_element_type=jnp.float32)
            own[chunk, pl.ds(group * group_wilds, group_wilds), :, pl.ds(which * width, width)] = (
                (scale[...] * total).astype(jnp.bfloat16).reshape(group_wilds, part, width)
            )

    tasks = [(group, chunk) for group in range(ROW_GROUPS) for chunk in range(HEAD_CHUNKS)]
    for time in range(len(tasks) + 2 * (seq_size - 1)):
        if time < len(tasks):
            project(*tasks[time])
            first_sends(*tasks[time])
        for step in range(seq_size - 1, 0, -1):
            if 0 <= time - 2 * step < len(tasks):
                forward(*tasks[time - 2 * step], step)

    for group in range(ROW_GROUPS):
        for off in range(1, mp_size):
            feature_copy(group, off, m).wait_send()
    for chunk in range(HEAD_CHUNKS):
        for piece in range(PIECES):
            pltpu.make_async_copy(
                own_slab(chunk, piece), slab(chunk, z, r, piece), o_sems.at[chunk, piece]
            ).wait()
            for step in range(seq_size):
                for way in range(2):
                    origin = origin_of(way, step)
                    if step < seq_size - 1:
                        pl.when(sends(way, step, piece))(
                            hop(way, step, chunk, piece, origin, step == 0).wait_send
                        )
                    if step == 0 and way == 1:
                        continue
                    for off in range(1, rep_size):
                        other = lax.rem(r - off + rep_size, rep_size)

                        @pl.when(twin_moves(way, step, piece))
                        def _():
                            twin(off, way, step, chunk, piece, origin, r, step == 0).wait_send()
                            twin(off, way, step, chunk, piece, origin, other, False).wait_recv()


def exchange(encoder_rows, norm_gain, key_weight, value_weight, slot_local):
    wild_total, part, part_width = encoder_rows.shape
    row_total = wild_total * part
    depth, inner = key_weight.shape
    seq_size, mp_size, rep_size = (lax.axis_size(name) for name in ("seq", "mp", "rep"))
    width = inner // HEAD_CHUNKS
    dma = pltpu.SemaphoreType.DMA
    peers_mp, peers_rep = max(mp_size - 1, 1), max(rep_size - 1, 1)
    whole = pl.BlockSpec(memory_space=pltpu.VMEM)
    place = pl.BlockSpec(memory_space=pl.ANY)
    return pl.pallas_call(
        functools.partial(exchange_kernel, (seq_size, mp_size, rep_size, slot_local, wild_total, part)),
        out_shape=jax.ShapeDtypeStruct(
            (HEAD_CHUNKS, seq_size, rep_size, wild_total, part, 2 * width), jnp.bfloat16
        ),
        in_specs=[place, whole, place, place],
        out_specs=place,
        scratch_shapes=[
            pltpu.VMEM((mp_size, row_total, part_width), jnp.bfloat16),
            pltpu.VMEM((HEAD_CHUNKS, 2, depth, width), jnp.bfloat16),
            pltpu.VMEM((row_total // ROW_GROUPS, depth), jnp.bfloat16),
            pltpu.VMEM((row_total // ROW_GROUPS, 1), jnp.float32),
            pltpu.VMEM((HEAD_CHUNKS, wild_total, part, 2 * width), jnp.bfloat16),
            dma((ROW_GROUPS,)),
            dma((HEAD_CHUNKS, 2)),
            dma((ROW_GROUPS, peers_mp)),
            dma((ROW_GROUPS, peers_mp)),
            dma((2, seq_size, HEAD_CHUNKS, PIECES)),
            dma((2, seq_size, HEAD_CHUNKS, PIECES)),
            dma((peers_rep, 2, seq_size, HEAD_CHUNKS, PIECES)),
            dma((peers_rep, 2, seq_size, HEAD_CHUNKS, PIECES)),
            dma((HEAD_CHUNKS, PIECES)),
        ],
        compiler_params=pltpu.CompilerParams(
            collective_id=0, has_side_effects=True, vmem_limit_bytes=40 << 20
        ),
    )(encoder_rows.reshape(row_total, part_width), norm_gain.astype(jnp.float32)[None, :], key_weight, value_weight)


def local(encoder_rows, norm_gain, key_weight, value_weight, queries, wild_lengths, variant_counts):
    wild_total = encoder_rows.shape[0]
    seq_size = lax.axis_size("seq")
    rep_size = lax.axis_size("rep")
    peer_total = seq_size * rep_size
    slot_local = queries.shape[0]
    slot_wild = wild_of_slots(variant_counts, peer_total * slot_local)
    own_index = lax.axis_index("seq") * rep_size + lax.axis_index("rep")
    own_wild = lax.dynamic_slice_in_dim(slot_wild, own_index * slot_local, slot_local, 0)
    wild_number = jnp.arange(wild_total, dtype=jnp.int32)
    own_lengths = jnp.sum(
        jnp.where(own_wild[:, None] == wild_number[None, :], wild_lengths[None, :], 0), axis=1
    )
    own_wild = jnp.minimum(own_wild, wild_total - 1)
    shared = exchange(encoder_rows, norm_gain, key_weight, value_weight, slot_local)
    gathered = shared.reshape((HEAD_CHUNKS, peer_total) + shared.shape[3:])
    return attend(own_wild, own_lengths, queries, gathered)


def solution(mesh):
    placed = (
        P("groups", ("seq", "rep"), "mp"),
        P(),
        P(None, "mp"),
        P(None, "mp"),
        P(("groups", "seq", "rep"), None, "mp"),
        P("groups"),
        P("groups"),
    )
    return jax.shard_map(
        local,
        mesh=mesh,
        in_specs=placed,
        out_specs=P(("groups", "seq", "rep"), None, "mp"),
        check_vma=False,
    )
```

```python
import functools

import jax
import jax.numpy as jnp
from jax import lax
from jax.experimental import pallas as pl
from jax.experimental.pallas import tpu as pltpu
from jax.sharding import PartitionSpec as P

D = 4096
HD = 64
LEN = 512
PAIR = 2 * HD
STEP_PAIRS = 4
HEAD_CHUNKS = 2
ROW_GROUPS = 2
PIECES = 4
COUNT_MIN = 4
COUNT_MAX = 12
MESH = pl.DeviceIdType.MESH


def wild_of_slots(variant_counts, slot_total):
    running_end = jnp.cumsum(variant_counts)
    slot_number = jnp.arange(slot_total, dtype=jnp.int32)
    return jnp.sum((running_end[None, :] <= slot_number[:, None]).astype(jnp.int32), axis=1)


def attend_kernel(wild_ref, length_ref, q_ref, k_ref, v_ref, o_ref):
    length = length_ref[pl.program_id(1)]
    items = [(pair, head) for pair in range(q_ref.shape[2] // PAIR) for head in range(2)]
    lane = lax.broadcasted_iota(jnp.int32, (LEN, PAIR), 1)

    def columns_of(pair):
        return pl.ds(pair * PAIR, PAIR)

    def score(pair, head):
        keys = k_ref[0, :, 0, :, columns_of(pair)].reshape(LEN, PAIR)
        query = q_ref[0, :, columns_of(pair)]
        own_lanes = lane < HD if head == 0 else lane >= HD
        return lax.dot_general(
            jnp.where(own_lanes, query, jnp.zeros_like(query)),
            keys,
            (((1,), (1,)), ((), ())),
            preferred_element_type=jnp.float32,
        )

    def attend_pairs(masked):
        following = score(*items[0])
        outs = []
        for at, (pair, head) in enumerate(items):
            scores = following
            if at + 1 < len(items):
                following = score(*items[at + 1])
            if masked:
                valid = lax.broadcasted_iota(jnp.int32, (LEN, LEN), 1) < length
                scores = jnp.where(valid, scores, jnp.float32(-1e30))
            maximum = jnp.max(scores, axis=1, keepdims=True)
            weights = jnp.exp(scores - maximum)
            inverse = 1.0 / jnp.sum(weights, axis=1, keepdims=True)
            probs = (weights * inverse).astype(jnp.bfloat16)
            values = v_ref[0, :, 0, :, columns_of(pair)].reshape(LEN, PAIR)
            outs.append(jnp.dot(probs, values, preferred_element_type=jnp.float32))
            if head == 1:
                out = jnp.where(lane < HD, outs[0], outs[1])
                outs = []
                if masked:
                    row = lax.broadcasted_iota(jnp.int32, (LEN, PAIR), 0)
                    out = jnp.where(row < length, out, 0.0)
                o_ref[0, :, columns_of(pair)] = out.astype(o_ref.dtype)

    pl.when(length < LEN)(lambda: attend_pairs(True))
    pl.when(length >= LEN)(lambda: attend_pairs(False))


def attend(own_wild, own_lengths, queries, gathered):
    slots, _, inner = queries.shape
    chunks, peers, _, part, double = gathered.shape
    block = min(STEP_PAIRS * PAIR, double // 2)
    per_chunk = double // 2 // block
    steps = chunks * per_chunk
    kv_block = (1, peers, 1, part, block)
    elements = slots * (inner // HD) * LEN * LEN
    return pl.pallas_call(
        attend_kernel,
        out_shape=jax.ShapeDtypeStruct(queries.shape, jnp.bfloat16),
        grid_spec=pltpu.PrefetchScalarGridSpec(
            num_scalar_prefetch=2,
            grid=(steps, slots),
            in_specs=[
                pl.BlockSpec((1, LEN, block), lambda h, s, w, n: (s, 0, h)),
                pl.BlockSpec(kv_block, lambda h, s, w, n: (h // per_chunk, 0, w[s], 0, h % per_chunk)),
                pl.BlockSpec(kv_block, lambda h, s, w, n: (h // per_chunk, 0, w[s], 0, per_chunk + h % per_chunk)),
            ],
            out_specs=pl.BlockSpec((1, LEN, block), lambda h, s, w, n: (s, 0, h)),
        ),
        compiler_params=pltpu.CompilerParams(vmem_limit_bytes=48 << 20),
        cost_estimate=pl.CostEstimate(
            flops=elements * 2 * PAIR * 2, transcendentals=elements, bytes_accessed=slots * LEN * inner * 8
        ),
    )(own_wild, own_lengths, queries, gathered, gathered)


def exchange_kernel(
    sizes, x_ref, gain_ref, kw_ref, vw_ref, out_ref, x_full, weights, gained, scale, own,
    x_sems, w_sems, x_send, x_recv, z_send, z_recv, r_send, r_recv, o_sems,
):
    seq_size, mp_size, rep_size, slot_local, wild_total, part = sizes
    z, m, r = lax.axis_index("seq"), lax.axis_index("mp"), lax.axis_index("rep")
    row_total, part_width = x_ref.shape
    width = kw_ref.shape[1] // HEAD_CHUNKS
    group_rows = row_total // ROW_GROUPS
    piece_wilds = wild_total // PIECES
    group_pieces = PIECES // ROW_GROUPS
    group_wilds = wild_total // ROW_GROUPS
    chip_slots = slot_local * rep_size
    total_slots = chip_slots * seq_size

    barrier = pltpu.get_barrier_semaphore()
    for off in range(1, mp_size):
        pl.semaphore_signal(barrier, 1, device_id={"mp": lax.rem(m + off, mp_size)}, device_id_type=MESH)
    for off in range(1, rep_size):
        pl.semaphore_signal(barrier, 1, device_id={"rep": lax.rem(r + off, rep_size)}, device_id_type=MESH)

    @pl.when(z < seq_size - 1)
    def _():
        pl.semaphore_signal(barrier, 1, device_id={"seq": z + 1}, device_id_type=MESH)

    @pl.when(z > 0)
    def _():
        pl.semaphore_signal(barrier, 1, device_id={"seq": z - 1}, device_id_type=MESH)

    def rows_of(group):
        return pl.ds(group * group_rows, group_rows)

    def own_copy(group):
        return pltpu.make_async_copy(
            x_ref.at[rows_of(group)], x_full.at[m, rows_of(group)], x_sems.at[group]
        )

    def weight_copy(chunk, which):
        ref = (kw_ref, vw_ref)[which]
        return pltpu.make_async_copy(
            ref.at[:, pl.ds(chunk * width, width)], weights.at[chunk, which], w_sems.at[chunk, which]
        )

    def feature_copy(group, off, sender):
        return pltpu.make_async_remote_copy(
            src_ref=x_ref.at[rows_of(group)],
            dst_ref=x_full.at[sender, rows_of(group)],
            send_sem=x_send.at[group, off - 1],
            recv_sem=x_recv.at[group, off - 1],
            device_id={"mp": lax.rem(m + off, mp_size)},
            device_id_type=MESH,
        )

    for group in range(ROW_GROUPS):
        own_copy(group).start()
    for chunk in range(HEAD_CHUNKS):
        for which in range(2):
            weight_copy(chunk, which).start()
    neighbours = (mp_size - 1) + (rep_size - 1) + jnp.where(z > 0, 1, 0) + jnp.where(z < seq_size - 1, 1, 0)
    pl.semaphore_wait(barrier, neighbours)
    for group in range(ROW_GROUPS):
        for off in range(1, mp_size):
            feature_copy(group, off, m).start()

    def lowest(piece):
        wild = piece * piece_wilds
        return max(COUNT_MIN * wild, total_slots - COUNT_MAX * (wild_total - wild))

    def highest(piece):
        wild = (piece + 1) * piece_wilds
        return min(COUNT_MAX * wild, total_slots - COUNT_MIN * (wild_total - wild))

    def wanted_right(chip, piece):
        return highest(piece) > chip * chip_slots

    def wanted_left(chip, piece):
        return lowest(piece) < (chip + 1) * chip_slots

    def slab(chunk, origin, core, piece):
        return out_ref.at[chunk, origin, core, pl.ds(piece * piece_wilds, piece_wilds)]

    def own_slab(chunk, piece):
        return own.at[chunk, pl.ds(piece * piece_wilds, piece_wilds)]

    def hop(way, step, chunk, piece, origin, from_own):
        ahead = z + 1 if way == 0 else z - 1
        return pltpu.make_async_remote_copy(
            src_ref=own_slab(chunk, piece) if from_own else slab(chunk, origin, r, piece),
            dst_ref=slab(chunk, origin, r, piece),
            send_sem=z_send.at[way, step, chunk, piece],
            recv_sem=z_recv.at[way, step, chunk, piece],
            device_id={"seq": ahead},
            device_id_type=MESH,
        )

    def twin(off, way, step, chunk, piece, origin, core, from_own):
        return pltpu.make_async_remote_copy(
            src_ref=own_slab(chunk, piece) if from_own else slab(chunk, origin, core, piece),
            dst_ref=slab(chunk, origin, core, piece),
            send_sem=r_send.at[off - 1, way, step, chunk, piece],
            recv_sem=r_recv.at[off - 1, way, step, chunk, piece],
            device_id={"rep": lax.rem(r + off, rep_size)},
            device_id_type=MESH,
        )

    def origin_of(way, step):
        return z - step if way == 0 else z + step

    def sends(way, step, piece):
        if way == 0:
            return (z - step >= 0) & (z < seq_size - 1) & wanted_right(z + 1, piece)
        return (z + step < seq_size) & (z > 0) & wanted_left(z - 1, piece)

    def arrives(way, step, piece):
        if way == 0:
            return (z - step >= 0) & wanted_right(z, piece)
        return (z + step < seq_size) & wanted_left(z, piece)

    def twin_moves(way, step, piece):
        near = wanted_right(z, piece) & wanted_left(z, piece)
        return near if step == 0 else near & arrives(way, step, piece)

    def first_sends(group, chunk):
        for piece in range(group * group_pieces, (group + 1) * group_pieces):
            for way in range(2):
                pl.when(sends(way, 0, piece))(hop(way, 0, chunk, piece, z, True).start)
            for off in range(1, rep_size):
                pl.when(twin_moves(0, 0, piece))(twin(off, 0, 0, chunk, piece, z, r, True).start)
            pltpu.make_async_copy(
                own_slab(chunk, piece), slab(chunk, z, r, piece), o_sems.at[chunk, piece]
            ).start()

    def forward(group, chunk, step):
        for piece in range(group * group_pieces, (group + 1) * group_pieces):
            for way in range(2):
                origin = origin_of(way, step)

                @pl.when(arrives(way, step, piece))
                def _():
                    hop(way, step - 1, chunk, piece, origin, False).wait_recv()

                if step < seq_size - 1:
                    pl.when(sends(way, step, piece))(hop(way, step, chunk, piece, origin, False).start)
                for off in range(1, rep_size):
                    pl.when(twin_moves(way, step, piece))(
                        twin(off, way, step, chunk, piece, origin, r, False).start
                    )

    def project(group, chunk):
        rows = rows_of(group)
        if chunk == 0:
            own_copy(group).wait()
            for off in range(1, mp_size):
                feature_copy(group, off, lax.rem(m - off + mp_size, mp_size)).wait_recv()
            squares = jnp.zeros((group_rows, 1), jnp.float32)
            for block in range(mp_size):
                columns = pl.ds(block * part_width, part_width)
                wide = x_full[block, rows, :].astype(jnp.float32)
                squares = squares + jnp.sum(wide * wide, axis=1, keepdims=True)
                gained[:, columns] = (wide * gain_ref[:, columns]).astype(jnp.bfloat16)
            scale[...] = lax.rsqrt(squares / D + 1e-06)
        for which in range(2):
            if group == 0:
                weight_copy(chunk, which).wait()
            total = jnp.dot(gained[...], weights[chunk, which], preferred_element_type=jnp.float32)
            own[chunk, pl.ds(group * group_wilds, group_wilds), :, pl.ds(which * width, width)] = (
                (scale[...] * total).astype(jnp.bfloat16).reshape(group_wilds, part, width)
            )

    tasks = [(group, chunk) for group in range(ROW_GROUPS) for chunk in range(HEAD_CHUNKS)]
    for time in range(len(tasks) + 2 * (seq_size - 1)):
        if time < len(tasks):
            project(*tasks[time])
            first_sends(*tasks[time])
        for step in range(seq_size - 1, 0, -1):
            if 0 <= time - 2 * step < len(tasks):
                forward(*tasks[time - 2 * step], step)

    for group in range(ROW_GROUPS):
        for off in range(1, mp_size):
            feature_copy(group, off, m).wait_send()
    for chunk in range(HEAD_CHUNKS):
        for piece in range(PIECES):
            pltpu.make_async_copy(
                own_slab(chunk, piece), slab(chunk, z, r, piece), o_sems.at[chunk, piece]
            ).wait()
            for step in range(seq_size):
                for way in range(2):
                    origin = origin_of(way, step)
                    if step < seq_size - 1:
                        pl.when(sends(way, step, piece))(
                            hop(way, step, chunk, piece, origin, step == 0).wait_send
                        )
                    if step == 0 and way == 1:
                        continue
                    for off in range(1, rep_size):
                        other = lax.rem(r - off + rep_size, rep_size)

                        @pl.when(twin_moves(way, step, piece))
                        def _():
                            twin(off, way, step, chunk, piece, origin, r, step == 0).wait_send()
                            twin(off, way, step, chunk, piece, origin, other, False).wait_recv()


def exchange(encoder_rows, norm_gain, key_weight, value_weight, slot_local):
    wild_total, part, part_width = encoder_rows.shape
    row_total = wild_total * part
    depth, inner = key_weight.shape
    seq_size, mp_size, rep_size = (lax.axis_size(name) for name in ("seq", "mp", "rep"))
    width = inner // HEAD_CHUNKS
    dma = pltpu.SemaphoreType.DMA
    peers_mp, peers_rep = max(mp_size - 1, 1), max(rep_size - 1, 1)
    whole = pl.BlockSpec(memory_space=pltpu.VMEM)
    place = pl.BlockSpec(memory_space=pl.ANY)
    return pl.pallas_call(
        functools.partial(exchange_kernel, (seq_size, mp_size, rep_size, slot_local, wild_total, part)),
        out_shape=jax.ShapeDtypeStruct(
            (HEAD_CHUNKS, seq_size, rep_size, wild_total, part, 2 * width), jnp.bfloat16
        ),
        in_specs=[place, whole, place, place],
        out_specs=place,
        scratch_shapes=[
            pltpu.VMEM((mp_size, row_total, part_width), jnp.bfloat16),
            pltpu.VMEM((HEAD_CHUNKS, 2, depth, width), jnp.bfloat16),
            pltpu.VMEM((row_total // ROW_GROUPS, depth), jnp.bfloat16),
            pltpu.VMEM((row_total // ROW_GROUPS, 1), jnp.float32),
            pltpu.VMEM((HEAD_CHUNKS, wild_total, part, 2 * width), jnp.bfloat16),
            dma((ROW_GROUPS,)),
            dma((HEAD_CHUNKS, 2)),
            dma((ROW_GROUPS, peers_mp)),
            dma((ROW_GROUPS, peers_mp)),
            dma((2, seq_size, HEAD_CHUNKS, PIECES)),
            dma((2, seq_size, HEAD_CHUNKS, PIECES)),
            dma((peers_rep, 2, seq_size, HEAD_CHUNKS, PIECES)),
            dma((peers_rep, 2, seq_size, HEAD_CHUNKS, PIECES)),
            dma((HEAD_CHUNKS, PIECES)),
        ],
        compiler_params=pltpu.CompilerParams(
            collective_id=0, has_side_effects=True, vmem_limit_bytes=40 << 20
        ),
    )(encoder_rows.reshape(row_total, part_width), norm_gain.astype(jnp.float32)[None, :], key_weight, value_weight)


def local(encoder_rows, norm_gain, key_weight, value_weight, queries, wild_lengths, variant_counts):
    wild_total = encoder_rows.shape[0]
    seq_size = lax.axis_size("seq")
    rep_size = lax.axis_size("rep")
    peer_total = seq_size * rep_size
    slot_local = queries.shape[0]
    slot_wild = wild_of_slots(variant_counts, peer_total * slot_local)
    own_index = lax.axis_index("seq") * rep_size + lax.axis_index("rep")
    own_wild = lax.dynamic_slice_in_dim(slot_wild, own_index * slot_local, slot_local, 0)
    wild_number = jnp.arange(wild_total, dtype=jnp.int32)
    own_lengths = jnp.sum(
        jnp.where(own_wild[:, None] == wild_number[None, :], wild_lengths[None, :], 0), axis=1
    )
    own_wild = jnp.minimum(own_wild, wild_total - 1)
    shared = exchange(encoder_rows, norm_gain, key_weight, value_weight, slot_local)
    gathered = shared.reshape((HEAD_CHUNKS, peer_total) + shared.shape[3:])
    return attend(own_wild, own_lengths, queries, gathered)


def solution(mesh):
    placed = (
        P("groups", ("seq", "rep"), "mp"),
        P(),
        P(None, "mp"),
        P(None, "mp"),
        P(("groups", "seq", "rep"), None, "mp"),
        P("groups"),
        P("groups"),
    )
    return jax.shard_map(
        local,
        mesh=mesh,
        in_specs=placed,
        out_specs=P(("groups", "seq", "rep"), None, "mp"),
        check_vma=False,
    )
```

```python
import functools

import jax
import jax.numpy as jnp
from jax import lax
from jax.experimental import pallas as pl
from jax.experimental.pallas import tpu as pltpu
from jax.sharding import PartitionSpec as P

D = 4096
HD = 64
LEN = 512
PAIR = 2 * HD
STEP_PAIRS = 4
HEAD_CHUNKS = 2
ROW_GROUPS = 4
PIECES = 4
COUNT_MIN = 4
COUNT_MAX = 12
MESH = pl.DeviceIdType.MESH


def wild_of_slots(variant_counts, slot_total):
    running_end = jnp.cumsum(variant_counts)
    slot_number = jnp.arange(slot_total, dtype=jnp.int32)
    return jnp.sum((running_end[None, :] <= slot_number[:, None]).astype(jnp.int32), axis=1)


def attend_kernel(wild_ref, length_ref, q_ref, k_ref, v_ref, o_ref):
    length = length_ref[pl.program_id(1)]
    items = [(pair, head) for pair in range(q_ref.shape[2] // PAIR) for head in range(2)]
    lane = lax.broadcasted_iota(jnp.int32, (LEN, PAIR), 1)

    def columns_of(pair):
        return pl.ds(pair * PAIR, PAIR)

    def score(pair, head):
        keys = k_ref[0, :, 0, :, columns_of(pair)].reshape(LEN, PAIR)
        query = q_ref[0, :, columns_of(pair)]
        own_lanes = lane < HD if head == 0 else lane >= HD
        return lax.dot_general(
            jnp.where(own_lanes, query, jnp.zeros_like(query)),
            keys,
            (((1,), (1,)), ((), ())),
            preferred_element_type=jnp.float32,
        )

    def attend_pairs(masked):
        following = score(*items[0])
        outs = []
        for at, (pair, head) in enumerate(items):
            scores = following
            if at + 1 < len(items):
                following = score(*items[at + 1])
            if masked:
                valid = lax.broadcasted_iota(jnp.int32, (LEN, LEN), 1) < length
                scores = jnp.where(valid, scores, jnp.float32(-1e30))
            maximum = jnp.max(scores, axis=1, keepdims=True)
            weights = jnp.exp(scores - maximum)
            inverse = 1.0 / jnp.sum(weights, axis=1, keepdims=True)
            probs = (weights * inverse).astype(jnp.bfloat16)
            values = v_ref[0, :, 0, :, columns_of(pair)].reshape(LEN, PAIR)
            outs.append(jnp.dot(probs, values, preferred_element_type=jnp.float32))
            if head == 1:
                out = jnp.where(lane < HD, outs[0], outs[1])
                outs = []
                if masked:
                    row = lax.broadcasted_iota(jnp.int32, (LEN, PAIR), 0)
                    out = jnp.where(row < length, out, 0.0)
                o_ref[0, :, columns_of(pair)] = out.astype(o_ref.dtype)

    pl.when(length < LEN)(lambda: attend_pairs(True))
    pl.when(length >= LEN)(lambda: attend_pairs(False))


def attend(own_wild, own_lengths, queries, gathered):
    slots, _, inner = queries.shape
    chunks, peers, _, part, double = gathered.shape
    block = min(STEP_PAIRS * PAIR, double // 2)
    per_chunk = double // 2 // block
    steps = chunks * per_chunk
    kv_block = (1, peers, 1, part, block)
    elements = slots * (inner // HD) * LEN * LEN
    return pl.pallas_call(
        attend_kernel,
        out_shape=jax.ShapeDtypeStruct(queries.shape, jnp.bfloat16),
        grid_spec=pltpu.PrefetchScalarGridSpec(
            num_scalar_prefetch=2,
            grid=(steps, slots),
            in_specs=[
                pl.BlockSpec((1, LEN, block), lambda h, s, w, n: (s, 0, h)),
                pl.BlockSpec(kv_block, lambda h, s, w, n: (h // per_chunk, 0, w[s], 0, h % per_chunk)),
                pl.BlockSpec(kv_block, lambda h, s, w, n: (h // per_chunk, 0, w[s], 0, per_chunk + h % per_chunk)),
            ],
            out_specs=pl.BlockSpec((1, LEN, block), lambda h, s, w, n: (s, 0, h)),
        ),
        compiler_params=pltpu.CompilerParams(vmem_limit_bytes=60 << 20),
        cost_estimate=pl.CostEstimate(
            flops=elements * 2 * PAIR * 2, transcendentals=elements, bytes_accessed=slots * LEN * inner * 8
        ),
    )(own_wild, own_lengths, queries, gathered, gathered)


def exchange_kernel(
    sizes, x_ref, gain_ref, kw_ref, vw_ref, out_ref, x_full, weights, gained, scale, own,
    x_sems, w_sems, x_send, x_recv, z_send, z_recv, r_send, r_recv, o_sems,
):
    seq_size, mp_size, rep_size, slot_local, wild_total, part = sizes
    z, m, r = lax.axis_index("seq"), lax.axis_index("mp"), lax.axis_index("rep")
    row_total, part_width = x_ref.shape
    width = kw_ref.shape[1] // HEAD_CHUNKS
    group_rows = row_total // ROW_GROUPS
    piece_wilds = wild_total // PIECES
    group_pieces = PIECES // ROW_GROUPS
    group_wilds = wild_total // ROW_GROUPS
    chip_slots = slot_local * rep_size
    total_slots = chip_slots * seq_size

    barrier = pltpu.get_barrier_semaphore()
    for off in range(1, mp_size):
        pl.semaphore_signal(barrier, 1, device_id={"mp": lax.rem(m + off, mp_size)}, device_id_type=MESH)
    for off in range(1, rep_size):
        pl.semaphore_signal(barrier, 1, device_id={"rep": lax.rem(r + off, rep_size)}, device_id_type=MESH)

    @pl.when(z < seq_size - 1)
    def _():
        pl.semaphore_signal(barrier, 1, device_id={"seq": z + 1}, device_id_type=MESH)

    @pl.when(z > 0)
    def _():
        pl.semaphore_signal(barrier, 1, device_id={"seq": z - 1}, device_id_type=MESH)

    def rows_of(group):
        return pl.ds(group * group_rows, group_rows)

    def own_copy(group):
        return pltpu.make_async_copy(
            x_ref.at[rows_of(group)], x_full.at[m, rows_of(group)], x_sems.at[group]
        )

    def weight_copy(chunk, which):
        ref = (kw_ref, vw_ref)[which]
        return pltpu.make_async_copy(
            ref.at[:, pl.ds(chunk * width, width)], weights.at[chunk, which], w_sems.at[chunk, which]
        )

    def feature_copy(group, off, sender):
        return pltpu.make_async_remote_copy(
            src_ref=x_ref.at[rows_of(group)],
            dst_ref=x_full.at[sender, rows_of(group)],
            send_sem=x_send.at[group, off - 1],
            recv_sem=x_recv.at[group, off - 1],
            device_id={"mp": lax.rem(m + off, mp_size)},
            device_id_type=MESH,
        )

    for group in range(ROW_GROUPS):
        own_copy(group).start()
    for chunk in range(HEAD_CHUNKS):
        for which in range(2):
            weight_copy(chunk, which).start()
    neighbours = (mp_size - 1) + (rep_size - 1) + jnp.where(z > 0, 1, 0) + jnp.where(z < seq_size - 1, 1, 0)
    pl.semaphore_wait(barrier, neighbours)
    for group in range(ROW_GROUPS):
        for off in range(1, mp_size):
            feature_copy(group, off, m).start()

    def lowest(piece):
        wild = piece * piece_wilds
        return max(COUNT_MIN * wild, total_slots - COUNT_MAX * (wild_total - wild))

    def highest(piece):
        wild = (piece + 1) * piece_wilds
        return min(COUNT_MAX * wild, total_slots - COUNT_MIN * (wild_total - wild))

    def wanted_right(chip, piece):
        return highest(piece) > chip * chip_slots

    def wanted_left(chip, piece):
        return lowest(piece) < (chip + 1) * chip_slots

    def slab(chunk, origin, core, piece):
        return out_ref.at[chunk, origin, core, pl.ds(piece * piece_wilds, piece_wilds)]

    def own_slab(chunk, piece):
        return own.at[chunk, pl.ds(piece * piece_wilds, piece_wilds)]

    def hop(way, step, chunk, piece, origin, from_own):
        ahead = z + 1 if way == 0 else z - 1
        return pltpu.make_async_remote_copy(
            src_ref=own_slab(chunk, piece) if from_own else slab(chunk, origin, r, piece),
            dst_ref=slab(chunk, origin, r, piece),
            send_sem=z_send.at[way, step, chunk, piece],
            recv_sem=z_recv.at[way, step, chunk, piece],
            device_id={"seq": ahead},
            device_id_type=MESH,
        )

    def twin(off, way, step, chunk, piece, origin, core, from_own):
        return pltpu.make_async_remote_copy(
            src_ref=own_slab(chunk, piece) if from_own else slab(chunk, origin, core, piece),
            dst_ref=slab(chunk, origin, core, piece),
            send_sem=r_send.at[off - 1, way, step, chunk, piece],
            recv_sem=r_recv.at[off - 1, way, step, chunk, piece],
            device_id={"rep": lax.rem(r + off, rep_size)},
            device_id_type=MESH,
        )

    def origin_of(way, step):
        return z - step if way == 0 else z + step

    def sends(way, step, piece):
        if way == 0:
            return (z - step >= 0) & (z < seq_size - 1) & wanted_right(z + 1, piece)
        return (z + step < seq_size) & (z > 0) & wanted_left(z - 1, piece)

    def arrives(way, step, piece):
        if way == 0:
            return (z - step >= 0) & wanted_right(z, piece)
        return (z + step < seq_size) & wanted_left(z, piece)

    def twin_moves(way, step, piece):
        near = wanted_right(z, piece) & wanted_left(z, piece)
        return near if step == 0 else near & arrives(way, step, piece)

    def first_sends(group, chunk):
        for piece in range(group * group_pieces, (group + 1) * group_pieces):
            for way in range(2):
                pl.when(sends(way, 0, piece))(hop(way, 0, chunk, piece, z, True).start)
            for off in range(1, rep_size):
                pl.when(twin_moves(0, 0, piece))(twin(off, 0, 0, chunk, piece, z, r, True).start)
            pltpu.make_async_copy(
                own_slab(chunk, piece), slab(chunk, z, r, piece), o_sems.at[chunk, piece]
            ).start()

    def forward(group, chunk, step):
        for piece in range(group * group_pieces, (group + 1) * group_pieces):
            for way in range(2):
                origin = origin_of(way, step)

                @pl.when(arrives(way, step, piece))
                def _():
                    hop(way, step - 1, chunk, piece, origin, False).wait_recv()

                if step < seq_size - 1:
                    pl.when(sends(way, step, piece))(hop(way, step, chunk, piece, origin, False).start)
                for off in range(1, rep_size):
                    pl.when(twin_moves(way, step, piece))(
                        twin(off, way, step, chunk, piece, origin, r, False).start
                    )

    def project(group, chunk):
        rows = rows_of(group)
        if chunk == 0:
            own_copy(group).wait()
            for off in range(1, mp_size):
                feature_copy(group, off, lax.rem(m - off + mp_size, mp_size)).wait_recv()
            squares = jnp.zeros((group_rows, 1), jnp.float32)
            for block in range(mp_size):
                columns = pl.ds(block * part_width, part_width)
                wide = x_full[block, rows, :].astype(jnp.float32)
                squares = squares + jnp.sum(wide * wide, axis=1, keepdims=True)
                gained[:, columns] = (wide * gain_ref[:, columns]).astype(jnp.bfloat16)
            scale[...] = lax.rsqrt(squares / D + 1e-06)
        for which in range(2):
            if group == 0:
                weight_copy(chunk, which).wait()
            total = jnp.dot(gained[...], weights[chunk, which], preferred_element_type=jnp.float32)
            own[chunk, pl.ds(group * group_wilds, group_wilds), :, pl.ds(which * width, width)] = (
                (scale[...] * total).astype(jnp.bfloat16).reshape(group_wilds, part, width)
            )

    tasks = [(group, chunk) for group in range(ROW_GROUPS) for chunk in range(HEAD_CHUNKS)]
    for time in range(len(tasks) + 2 * (seq_size - 1)):
        if time < len(tasks):
            project(*tasks[time])
            first_sends(*tasks[time])
        for step in range(seq_size - 1, 0, -1):
            if 0 <= time - 2 * step < len(tasks):
                forward(*tasks[time - 2 * step], step)

    for group in range(ROW_GROUPS):
        for off in range(1, mp_size):
            feature_copy(group, off, m).wait_send()
    for chunk in range(HEAD_CHUNKS):
        for piece in range(PIECES):
            pltpu.make_async_copy(
                own_slab(chunk, piece), slab(chunk, z, r, piece), o_sems.at[chunk, piece]
            ).wait()
            for step in range(seq_size):
                for way in range(2):
                    origin = origin_of(way, step)
                    if step < seq_size - 1:
                        pl.when(sends(way, step, piece))(
                            hop(way, step, chunk, piece, origin, step == 0).wait_send
                        )
                    if step == 0 and way == 1:
                        continue
                    for off in range(1, rep_size):
                        other = lax.rem(r - off + rep_size, rep_size)

                        @pl.when(twin_moves(way, step, piece))
                        def _():
                            twin(off, way, step, chunk, piece, origin, r, step == 0).wait_send()
                            twin(off, way, step, chunk, piece, origin, other, False).wait_recv()


def exchange(encoder_rows, norm_gain, key_weight, value_weight, slot_local):
    wild_total, part, part_width = encoder_rows.shape
    row_total = wild_total * part
    depth, inner = key_weight.shape
    seq_size, mp_size, rep_size = (lax.axis_size(name) for name in ("seq", "mp", "rep"))
    width = inner // HEAD_CHUNKS
    dma = pltpu.SemaphoreType.DMA
    peers_mp, peers_rep = max(mp_size - 1, 1), max(rep_size - 1, 1)
    whole = pl.BlockSpec(memory_space=pltpu.VMEM)
    place = pl.BlockSpec(memory_space=pl.ANY)
    return pl.pallas_call(
        functools.partial(exchange_kernel, (seq_size, mp_size, rep_size, slot_local, wild_total, part)),
        out_shape=jax.ShapeDtypeStruct(
            (HEAD_CHUNKS, seq_size, rep_size, wild_total, part, 2 * width), jnp.bfloat16
        ),
        in_specs=[place, whole, place, place],
        out_specs=place,
        scratch_shapes=[
            pltpu.VMEM((mp_size, row_total, part_width), jnp.bfloat16),
            pltpu.VMEM((HEAD_CHUNKS, 2, depth, width), jnp.bfloat16),
            pltpu.VMEM((row_total // ROW_GROUPS, depth), jnp.bfloat16),
            pltpu.VMEM((row_total // ROW_GROUPS, 1), jnp.float32),
            pltpu.VMEM((HEAD_CHUNKS, wild_total, part, 2 * width), jnp.bfloat16),
            dma((ROW_GROUPS,)),
            dma((HEAD_CHUNKS, 2)),
            dma((ROW_GROUPS, peers_mp)),
            dma((ROW_GROUPS, peers_mp)),
            dma((2, seq_size, HEAD_CHUNKS, PIECES)),
            dma((2, seq_size, HEAD_CHUNKS, PIECES)),
            dma((peers_rep, 2, seq_size, HEAD_CHUNKS, PIECES)),
            dma((peers_rep, 2, seq_size, HEAD_CHUNKS, PIECES)),
            dma((HEAD_CHUNKS, PIECES)),
        ],
        compiler_params=pltpu.CompilerParams(
            collective_id=0, has_side_effects=True, vmem_limit_bytes=40 << 20
        ),
    )(encoder_rows.reshape(row_total, part_width), norm_gain.astype(jnp.float32)[None, :], key_weight, value_weight)


def local(encoder_rows, norm_gain, key_weight, value_weight, queries, wild_lengths, variant_counts):
    wild_total = encoder_rows.shape[0]
    seq_size = lax.axis_size("seq")
    rep_size = lax.axis_size("rep")
    peer_total = seq_size * rep_size
    slot_local = queries.shape[0]
    slot_wild = wild_of_slots(variant_counts, peer_total * slot_local)
    own_index = lax.axis_index("seq") * rep_size + lax.axis_index("rep")
    own_wild = lax.dynamic_slice_in_dim(slot_wild, own_index * slot_local, slot_local, 0)
    wild_number = jnp.arange(wild_total, dtype=jnp.int32)
    own_lengths = jnp.sum(
        jnp.where(own_wild[:, None] == wild_number[None, :], wild_lengths[None, :], 0), axis=1
    )
    own_wild = jnp.minimum(own_wild, wild_total - 1)
    shared = exchange(encoder_rows, norm_gain, key_weight, value_weight, slot_local)
    gathered = shared.reshape((HEAD_CHUNKS, peer_total) + shared.shape[3:])
    return attend(own_wild, own_lengths, queries, gathered)


def solution(mesh):
    placed = (
        P("groups", ("seq", "rep"), "mp"),
        P(),
        P(None, "mp"),
        P(None, "mp"),
        P(("groups", "seq", "rep"), None, "mp"),
        P("groups"),
        P("groups"),
    )
    return jax.shard_map(
        local,
        mesh=mesh,
        in_specs=placed,
        out_specs=P(("groups", "seq", "rep"), None, "mp"),
        check_vma=False,
    )
```

```python
import functools

import jax
import jax.numpy as jnp
from jax import lax
from jax.experimental import pallas as pl
from jax.experimental.pallas import tpu as pltpu
from jax.sharding import PartitionSpec as P

D = 4096
HD = 64
LEN = 512
PAIR = 2 * HD
STEP_PAIRS = 4
HEAD_CHUNKS = 2
ROW_GROUPS = 4
PIECES = 4
COUNT_MIN = 4
COUNT_MAX = 12
MESH = pl.DeviceIdType.MESH


def wild_of_slots(variant_counts, slot_total):
    running_end = jnp.cumsum(variant_counts)
    slot_number = jnp.arange(slot_total, dtype=jnp.int32)
    return jnp.sum((running_end[None, :] <= slot_number[:, None]).astype(jnp.int32), axis=1)


def attend_kernel(wild_ref, length_ref, q_ref, k_ref, v_ref, o_ref):
    length = length_ref[pl.program_id(1)]
    items = [(pair, head) for pair in range(q_ref.shape[2] // PAIR) for head in range(2)]
    lane = lax.broadcasted_iota(jnp.int32, (LEN, PAIR), 1)

    def columns_of(pair):
        return pl.ds(pair * PAIR, PAIR)

    def score(pair, head):
        keys = k_ref[0, :, 0, :, columns_of(pair)].reshape(LEN, PAIR)
        query = q_ref[0, :, columns_of(pair)]
        own_lanes = lane < HD if head == 0 else lane >= HD
        return lax.dot_general(
            jnp.where(own_lanes, query, jnp.zeros_like(query)),
            keys,
            (((1,), (1,)), ((), ())),
            preferred_element_type=jnp.float32,
        )

    def attend_pairs(masked):
        following = score(*items[0])
        outs = []
        for at, (pair, head) in enumerate(items):
            scores = following
            if at + 1 < len(items):
                following = score(*items[at + 1])
            if masked:
                valid = lax.broadcasted_iota(jnp.int32, (LEN, LEN), 1) < length
                scores = jnp.where(valid, scores, jnp.float32(-1e30))
            maximum = jnp.max(scores, axis=1, keepdims=True)
            weights = jnp.exp(scores - maximum)
            inverse = 1.0 / jnp.sum(weights, axis=1, keepdims=True)
            probs = (weights * inverse).astype(jnp.bfloat16)
            values = v_ref[0, :, 0, :, columns_of(pair)].reshape(LEN, PAIR)
            outs.append(jnp.dot(probs, values, preferred_element_type=jnp.float32))
            if head == 1:
                out = jnp.where(lane < HD, outs[0], outs[1])
                outs = []
                if masked:
                    row = lax.broadcasted_iota(jnp.int32, (LEN, PAIR), 0)
                    out = jnp.where(row < length, out, 0.0)
                o_ref[0, :, columns_of(pair)] = out.astype(o_ref.dtype)

    pl.when(length < LEN)(lambda: attend_pairs(True))
    pl.when(length >= LEN)(lambda: attend_pairs(False))


def attend(own_wild, own_lengths, queries, gathered):
    slots, _, inner = queries.shape
    chunks, peers, _, part, double = gathered.shape
    block = min(STEP_PAIRS * PAIR, double // 2)
    per_chunk = double // 2 // block
    steps = chunks * per_chunk
    kv_block = (1, peers, 1, part, block)
    elements = slots * (inner // HD) * LEN * LEN
    return pl.pallas_call(
        attend_kernel,
        out_shape=jax.ShapeDtypeStruct(queries.shape, jnp.bfloat16),
        grid_spec=pltpu.PrefetchScalarGridSpec(
            num_scalar_prefetch=2,
            grid=(steps, slots),
            in_specs=[
                pl.BlockSpec((1, LEN, block), lambda h, s, w, n: (s, 0, h)),
                pl.BlockSpec(kv_block, lambda h, s, w, n: (h // per_chunk, 0, w[s], 0, h % per_chunk)),
                pl.BlockSpec(kv_block, lambda h, s, w, n: (h // per_chunk, 0, w[s], 0, per_chunk + h % per_chunk)),
            ],
            out_specs=pl.BlockSpec((1, LEN, block), lambda h, s, w, n: (s, 0, h)),
        ),
        compiler_params=pltpu.CompilerParams(vmem_limit_bytes=32 << 20),
        cost_estimate=pl.CostEstimate(
            flops=elements * 2 * PAIR * 2, transcendentals=elements, bytes_accessed=slots * LEN * inner * 8
        ),
    )(own_wild, own_lengths, queries, gathered, gathered)


def exchange_kernel(
    sizes, x_ref, gain_ref, kw_ref, vw_ref, out_ref, x_full, weights, gained, scale, own,
    x_sems, w_sems, x_send, x_recv, z_send, z_recv, r_send, r_recv, o_sems,
):
    seq_size, mp_size, rep_size, slot_local, wild_total, part = sizes
    z, m, r = lax.axis_index("seq"), lax.axis_index("mp"), lax.axis_index("rep")
    row_total, part_width = x_ref.shape
    width = kw_ref.shape[1] // HEAD_CHUNKS
    group_rows = row_total // ROW_GROUPS
    piece_wilds = wild_total // PIECES
    group_pieces = PIECES // ROW_GROUPS
    group_wilds = wild_total // ROW_GROUPS
    chip_slots = slot_local * rep_size
    total_slots = chip_slots * seq_size

    barrier = pltpu.get_barrier_semaphore()
    for off in range(1, mp_size):
        pl.semaphore_signal(barrier, 1, device_id={"mp": lax.rem(m + off, mp_size)}, device_id_type=MESH)
    for off in range(1, rep_size):
        pl.semaphore_signal(barrier, 1, device_id={"rep": lax.rem(r + off, rep_size)}, device_id_type=MESH)

    @pl.when(z < seq_size - 1)
    def _():
        pl.semaphore_signal(barrier, 1, device_id={"seq": z + 1}, device_id_type=MESH)

    @pl.when(z > 0)
    def _():
        pl.semaphore_signal(barrier, 1, device_id={"seq": z - 1}, device_id_type=MESH)

    def rows_of(group):
        return pl.ds(group * group_rows, group_rows)

    def own_copy(group):
        return pltpu.make_async_copy(
            x_ref.at[rows_of(group)], x_full.at[m, rows_of(group)], x_sems.at[group]
        )

    def weight_copy(chunk, which):
        ref = (kw_ref, vw_ref)[which]
        return pltpu.make_async_copy(
            ref.at[:, pl.ds(chunk * width, width)], weights.at[chunk, which], w_sems.at[chunk, which]
        )

    def feature_copy(group, off, sender):
        return pltpu.make_async_remote_copy(
            src_ref=x_ref.at[rows_of(group)],
            dst_ref=x_full.at[sender, rows_of(group)],
            send_sem=x_send.at[group, off - 1],
            recv_sem=x_recv.at[group, off - 1],
            device_id={"mp": lax.rem(m + off, mp_size)},
            device_id_type=MESH,
        )

    for group in range(ROW_GROUPS):
        own_copy(group).start()
    for chunk in range(HEAD_CHUNKS):
        for which in range(2):
            weight_copy(chunk, which).start()
    neighbours = (mp_size - 1) + (rep_size - 1) + jnp.where(z > 0, 1, 0) + jnp.where(z < seq_size - 1, 1, 0)
    pl.semaphore_wait(barrier, neighbours)
    for group in range(ROW_GROUPS):
        for off in range(1, mp_size):
            feature_copy(group, off, m).start()

    def lowest(piece):
        wild = piece * piece_wilds
        return max(COUNT_MIN * wild, total_slots - COUNT_MAX * (wild_total - wild))

    def highest(piece):
        wild = (piece + 1) * piece_wilds
        return min(COUNT_MAX * wild, total_slots - COUNT_MIN * (wild_total - wild))

    def wanted_right(chip, piece):
        return highest(piece) > chip * chip_slots

    def wanted_left(chip, piece):
        return lowest(piece) < (chip + 1) * chip_slots

    def slab(chunk, origin, core, piece):
        return out_ref.at[chunk, origin, core, pl.ds(piece * piece_wilds, piece_wilds)]

    def own_slab(chunk, piece):
        return own.at[chunk, pl.ds(piece * piece_wilds, piece_wilds)]

    def hop(way, step, chunk, piece, origin, from_own):
        ahead = z + 1 if way == 0 else z - 1
        return pltpu.make_async_remote_copy(
            src_ref=own_slab(chunk, piece) if from_own else slab(chunk, origin, r, piece),
            dst_ref=slab(chunk, origin, r, piece),
            send_sem=z_send.at[way, step, chunk, piece],
            recv_sem=z_recv.at[way, step, chunk, piece],
            device_id={"seq": ahead},
            device_id_type=MESH,
        )

    def twin(off, way, step, chunk, piece, origin, core, from_own):
        return pltpu.make_async_remote_copy(
            src_ref=own_slab(chunk, piece) if from_own else slab(chunk, origin, core, piece),
            dst_ref=slab(chunk, origin, core, piece),
            send_sem=r_send.at[off - 1, way, step, chunk, piece],
            recv_sem=r_recv.at[off - 1, way, step, chunk, piece],
            device_id={"rep": lax.rem(r + off, rep_size)},
            device_id_type=MESH,
        )

    def origin_of(way, step):
        return z - step if way == 0 else z + step

    def sends(way, step, piece):
        if way == 0:
            return (z - step >= 0) & (z < seq_size - 1) & wanted_right(z + 1, piece)
        return (z + step < seq_size) & (z > 0) & wanted_left(z - 1, piece)

    def arrives(way, step, piece):
        if way == 0:
            return (z - step >= 0) & wanted_right(z, piece)
        return (z + step < seq_size) & wanted_left(z, piece)

    def twin_moves(way, step, piece):
        near = wanted_right(z, piece) & wanted_left(z, piece)
        return near if step == 0 else near & arrives(way, step, piece)

    def first_sends(group, chunk):
        for piece in range(group * group_pieces, (group + 1) * group_pieces):
            for way in range(2):
                pl.when(sends(way, 0, piece))(hop(way, 0, chunk, piece, z, True).start)
            for off in range(1, rep_size):
                pl.when(twin_moves(0, 0, piece))(twin(off, 0, 0, chunk, piece, z, r, True).start)
            pltpu.make_async_copy(
                own_slab(chunk, piece), slab(chunk, z, r, piece), o_sems.at[chunk, piece]
            ).start()

    def forward(group, chunk, step):
        for piece in range(group * group_pieces, (group + 1) * group_pieces):
            for way in range(2):
                origin = origin_of(way, step)

                @pl.when(arrives(way, step, piece))
                def _():
                    hop(way, step - 1, chunk, piece, origin, False).wait_recv()

                if step < seq_size - 1:
                    pl.when(sends(way, step, piece))(hop(way, step, chunk, piece, origin, False).start)
                for off in range(1, rep_size):
                    pl.when(twin_moves(way, step, piece))(
                        twin(off, way, step, chunk, piece, origin, r, False).start
                    )

    def project(group, chunk):
        rows = rows_of(group)
        if chunk == 0:
            own_copy(group).wait()
            for off in range(1, mp_size):
                feature_copy(group, off, lax.rem(m - off + mp_size, mp_size)).wait_recv()
            squares = jnp.zeros((group_rows, 1), jnp.float32)
            for block in range(mp_size):
                columns = pl.ds(block * part_width, part_width)
                wide = x_full[block, rows, :].astype(jnp.float32)
                squares = squares + jnp.sum(wide * wide, axis=1, keepdims=True)
                gained[:, columns] = (wide * gain_ref[:, columns]).astype(jnp.bfloat16)
            scale[...] = lax.rsqrt(squares / D + 1e-06)
        for which in range(2):
            if group == 0:
                weight_copy(chunk, which).wait()
            total = jnp.dot(gained[...], weights[chunk, which], preferred_element_type=jnp.float32)
            own[chunk, pl.ds(group * group_wilds, group_wilds), :, pl.ds(which * width, width)] = (
                (scale[...] * total).astype(jnp.bfloat16).reshape(group_wilds, part, width)
            )

    tasks = [(group, chunk) for group in range(ROW_GROUPS) for chunk in range(HEAD_CHUNKS)]
    for time in range(len(tasks) + 2 * (seq_size - 1)):
        if time < len(tasks):
            project(*tasks[time])
            first_sends(*tasks[time])
        for step in range(seq_size - 1, 0, -1):
            if 0 <= time - 2 * step < len(tasks):
                forward(*tasks[time - 2 * step], step)

    for group in range(ROW_GROUPS):
        for off in range(1, mp_size):
            feature_copy(group, off, m).wait_send()
    for chunk in range(HEAD_CHUNKS):
        for piece in range(PIECES):
            pltpu.make_async_copy(
                own_slab(chunk, piece), slab(chunk, z, r, piece), o_sems.at[chunk, piece]
            ).wait()
            for step in range(seq_size):
                for way in range(2):
                    origin = origin_of(way, step)
                    if step < seq_size - 1:
                        pl.when(sends(way, step, piece))(
                            hop(way, step, chunk, piece, origin, step == 0).wait_send
                        )
                    if step == 0 and way == 1:
                        continue
                    for off in range(1, rep_size):
                        other = lax.rem(r - off + rep_size, rep_size)

                        @pl.when(twin_moves(way, step, piece))
                        def _():
                            twin(off, way, step, chunk, piece, origin, r, step == 0).wait_send()
                            twin(off, way, step, chunk, piece, origin, other, False).wait_recv()


def exchange(encoder_rows, norm_gain, key_weight, value_weight, slot_local):
    wild_total, part, part_width = encoder_rows.shape
    row_total = wild_total * part
    depth, inner = key_weight.shape
    seq_size, mp_size, rep_size = (lax.axis_size(name) for name in ("seq", "mp", "rep"))
    width = inner // HEAD_CHUNKS
    dma = pltpu.SemaphoreType.DMA
    peers_mp, peers_rep = max(mp_size - 1, 1), max(rep_size - 1, 1)
    whole = pl.BlockSpec(memory_space=pltpu.VMEM)
    place = pl.BlockSpec(memory_space=pl.ANY)
    return pl.pallas_call(
        functools.partial(exchange_kernel, (seq_size, mp_size, rep_size, slot_local, wild_total, part)),
        out_shape=jax.ShapeDtypeStruct(
            (HEAD_CHUNKS, seq_size, rep_size, wild_total, part, 2 * width), jnp.bfloat16
        ),
        in_specs=[place, whole, place, place],
        out_specs=place,
        scratch_shapes=[
            pltpu.VMEM((mp_size, row_total, part_width), jnp.bfloat16),
            pltpu.VMEM((HEAD_CHUNKS, 2, depth, width), jnp.bfloat16),
            pltpu.VMEM((row_total // ROW_GROUPS, depth), jnp.bfloat16),
            pltpu.VMEM((row_total // ROW_GROUPS, 1), jnp.float32),
            pltpu.VMEM((HEAD_CHUNKS, wild_total, part, 2 * width), jnp.bfloat16),
            dma((ROW_GROUPS,)),
            dma((HEAD_CHUNKS, 2)),
            dma((ROW_GROUPS, peers_mp)),
            dma((ROW_GROUPS, peers_mp)),
            dma((2, seq_size, HEAD_CHUNKS, PIECES)),
            dma((2, seq_size, HEAD_CHUNKS, PIECES)),
            dma((peers_rep, 2, seq_size, HEAD_CHUNKS, PIECES)),
            dma((peers_rep, 2, seq_size, HEAD_CHUNKS, PIECES)),
            dma((HEAD_CHUNKS, PIECES)),
        ],
        compiler_params=pltpu.CompilerParams(
            collective_id=0, has_side_effects=True, vmem_limit_bytes=40 << 20
        ),
    )(encoder_rows.reshape(row_total, part_width), norm_gain.astype(jnp.float32)[None, :], key_weight, value_weight)


def local(encoder_rows, norm_gain, key_weight, value_weight, queries, wild_lengths, variant_counts):
    wild_total = encoder_rows.shape[0]
    seq_size = lax.axis_size("seq")
    rep_size = lax.axis_size("rep")
    peer_total = seq_size * rep_size
    slot_local = queries.shape[0]
    slot_wild = wild_of_slots(variant_counts, peer_total * slot_local)
    own_index = lax.axis_index("seq") * rep_size + lax.axis_index("rep")
    own_wild = lax.dynamic_slice_in_dim(slot_wild, own_index * slot_local, slot_local, 0)
    wild_number = jnp.arange(wild_total, dtype=jnp.int32)
    own_lengths = jnp.sum(
        jnp.where(own_wild[:, None] == wild_number[None, :], wild_lengths[None, :], 0), axis=1
    )
    own_wild = jnp.minimum(own_wild, wild_total - 1)
    shared = exchange(encoder_rows, norm_gain, key_weight, value_weight, slot_local)
    gathered = shared.reshape((HEAD_CHUNKS, peer_total) + shared.shape[3:])
    return attend(own_wild, own_lengths, queries, gathered)


def solution(mesh):
    placed = (
        P("groups", ("seq", "rep"), "mp"),
        P(),
        P(None, "mp"),
        P(None, "mp"),
        P(("groups", "seq", "rep"), None, "mp"),
        P("groups"),
        P("groups"),
    )
    return jax.shard_map(
        local,
        mesh=mesh,
        in_specs=placed,
        out_specs=P(("groups", "seq", "rep"), None, "mp"),
        check_vma=False,
    )
```
